32 devices in a mesh: traj: 8 (over z, core), amp: 4 (over y, x).
Axes of the slice: x: 2, y: 2, z: 4, core: 2. Of those that a mesh axis runs over, the one named last changes fastest.
Arguments:
- amplitudes: float32 [8, 2, 524288], P('traj', None, 'amp'), parts along dimension 0, may hold values from -6 to 6
- couplings: float32 [18], replicated, may hold values from 0.5 to 2
- fields: float32 [19], replicated, may hold values from 0.5 to 2
- decays: float32 [19], replicated, may hold values from 0.2 to 2
- channel: int32 [8], P('traj'), parts along dimension 0, may hold values from 0 to 19
Outputs:
- evolved_state: float32 [8, 2, 524288], P('traj', None, 'amp'), parts along dimension 0
The draws below stay inside these ranges and needn't reach their ends.
There are 8 independent parts, one for each index of `traj`. The reference program is written for one: setup_inputs(seed, part) draws one part's arguments, and reference() takes and returns one part's arrays. A program takes and returns all parts, laid end to end along the dimension named above; an argument that names none is the same for every part. Nothing has to cross between parts.
Inputs may be any that keep to these rules, and one draw needn't show every extreme that they name: `channel`: the value 19 means that the trajectory does not jump.
All inputs are finite; a program needn't handle non-finite values.
Results may differ from the reference program's by a relative error of at most 0.0003.
Values sent between devices are 32-bit elements; how exact they have to be, the bound alone decides.
A program may use at most 256 MiB of HBM per device.

```python
import math
import jax
import jax.numpy as jnp
from jax import lax

SPINS = 19
KRYLOV = 8
TRAJ = 1
AMPS = 524288


def steps_of(rng, dims, cuts, smallest, largest):
    def one(dim, shards_of):
        steps = jax.random.uniform(jax.random.fold_in(jax.random.fold_in(rng, 6), dim), (shards_of,), jnp.float32, smallest / len(cuts), largest / len(cuts))
        return jnp.repeat(jnp.exp(steps), dims[dim] // shards_of).reshape((-1,) + (1,) * (len(dims) - dim - 1))

    factor_of = one(*cuts[0])
    for cut in cuts[1:]:
        factor_of = factor_of * one(*cut)
    return factor_of


def noise(stream_key, dims, deviation, most, pieces=(), kind=jnp.bfloat16):
    drawn = jax.random.normal(stream_key, dims, jnp.float32) * deviation
    if len(pieces) > 0:
        drawn = steps_of(stream_key, dims, pieces, -0.22, 0.18) * drawn
    return jnp.clip(drawn, min=-most, max=most).astype(kind)


def setup_inputs(seed: int = 0, part: int = 0) -> dict:
    streams_of = jax.random.split(jax.random.key(seed), 6)
    own_keys = jax.random.split(jax.random.fold_in(streams_of[5], part), 6)
    amplitudes = noise(own_keys[0], (TRAJ, 2, AMPS), 1.0, 6.0, ((2, 4),), jnp.float32)
    couplings = jnp.clip(jnp.exp(jax.random.uniform(streams_of[1], (SPINS - 1,), jnp.float32, math.log(0.5), math.log(2.0))), 0.5, 2.0)
    fields = jnp.clip(jnp.exp(jax.random.uniform(streams_of[2], (SPINS,), jnp.float32, math.log(0.5), math.log(2.0))), 0.5, 2.0)
    decays = jnp.clip(jnp.exp(jax.random.uniform(streams_of[3], (SPINS,), jnp.float32, math.log(0.2), math.log(2.0))), 0.2, 2.0)
    channel = jax.random.randint(own_keys[4], (TRAJ,), 0, SPINS + 1).astype(jnp.int32)
    return dict(amplitudes=amplitudes, couplings=couplings, fields=fields, decays=decays, channel=channel)


time_step = 0.7
squarings = 8
taylor_order = 10
highest = lax.Precision.HIGHEST

def flip_spin(vector, spin_pos):
    leading = vector.shape[:-1]
    length = vector.shape[-1]
    parted = vector.reshape(leading + (length >> spin_pos + 1, 2, 1 << spin_pos))
    return jnp.flip(parted, axis=len(leading) + 1).reshape(vector.shape)

def apply_heff(vector, fields, diag_real, diag_imag):
    flipped = jnp.zeros_like(vector)
    for spin_pos in range(SPINS):
        flipped = flipped + fields[spin_pos] * flip_spin(vector, spin_pos)
    real_part = vector[:, 0]
    imag_part = vector[:, 1]
    out_real = diag_real * real_part - diag_imag * imag_part - flipped[:, 0]
    out_imag = diag_real * imag_part + diag_imag * real_part - flipped[:, 1]
    return jnp.stack([out_real, out_imag], axis=1)

def krylov_weights(scale_norm, hess_real, hess_imag):
    a_real = time_step * hess_imag
    a_imag = -time_step * hess_real
    upper_half = jnp.concatenate([a_real, -a_imag], axis=2)
    lower_half = jnp.concatenate([a_imag, a_real], axis=2)
    scaled = jnp.concatenate([upper_half, lower_half], axis=1) / 2.0 ** squarings
    identity = jnp.broadcast_to(jnp.eye(2 * KRYLOV, dtype=jnp.float32), scaled.shape)
    series = identity
    for degree in range(taylor_order, 0, -1):
        series = identity + jnp.einsum('tij,tjk->tik', scaled, series, precision=highest) / degree
    for repeat in range(squarings):
        series = jnp.einsum('tij,tjk->tik', series, series, precision=highest)
    first_column = series[:, :, 0] * scale_norm[:, None]
    return (first_column[:, :KRYLOV], first_column[:, KRYLOV:])

def reference(amplitudes, couplings, fields, decays, channel):
    traj_count = amplitudes.shape[0]
    position = jnp.arange(AMPS, dtype=jnp.int32)
    occupation = [(position >> spin_pos & 1).astype(jnp.float32) for spin_pos in range(SPINS)]
    diag_real = jnp.zeros((AMPS,), jnp.float32)
    for spin_pos in range(SPINS - 1):
        diag_real = diag_real - couplings[spin_pos] * (1.0 - 2.0 * occupation[spin_pos]) * (1.0 - 2.0 * occupation[spin_pos + 1])
    diag_imag = jnp.zeros((AMPS,), jnp.float32)
    for spin_pos in range(SPINS):
        diag_imag = diag_imag - 0.5 * decays[spin_pos] * occupation[spin_pos]
    scale_norm = jnp.sqrt(lax.optimization_barrier(jnp.sum(amplitudes * amplitudes, axis=(1, 2))))
    krylov_basis = [amplitudes / scale_norm[:, None, None]]
    hess_real = jnp.zeros((traj_count, KRYLOV, KRYLOV), jnp.float32)
    hess_imag = jnp.zeros((traj_count, KRYLOV, KRYLOV), jnp.float32)
    for column in range(KRYLOV):
        applied = apply_heff(krylov_basis[column], fields, diag_real, diag_imag)
        stacked = jnp.stack(krylov_basis, axis=1)
        swapped = jnp.stack([applied[:, 1], -applied[:, 0]], axis=1)
        proj_real = jnp.einsum('tkca,tca->tk', stacked, applied, precision=highest)
        proj_imag = jnp.einsum('tkca,tca->tk', stacked, swapped, precision=highest)
        hess_real = hess_real.at[:, :column + 1, column].set(proj_real)
        hess_imag = hess_imag.at[:, :column + 1, column].set(proj_imag)
        if column + 1 < KRYLOV:
            comb_real = jnp.einsum('tk,tka->ta', proj_real, stacked[:, :, 0], precision=highest) - jnp.einsum('tk,tka->ta', proj_imag, stacked[:, :, 1], precision=highest)
            comb_imag = jnp.einsum('tk,tka->ta', proj_real, stacked[:, :, 1], precision=highest) + jnp.einsum('tk,tka->ta', proj_imag, stacked[:, :, 0], precision=highest)
            residual = applied - jnp.stack([comb_real, comb_imag], axis=1)
            column_norm = jnp.sqrt(lax.optimization_barrier(jnp.sum(residual * residual, axis=(1, 2))))
            hess_real = hess_real.at[:, column + 1, column].set(column_norm)
            krylov_basis.append(residual / column_norm[:, None, None])
    weights_real, weights_imag = krylov_weights(scale_norm, hess_real, hess_imag)
    stacked = jnp.stack(krylov_basis, axis=1)
    new_real = jnp.einsum('tk,tka->ta', weights_real, stacked[:, :, 0], precision=highest) - jnp.einsum('tk,tka->ta', weights_imag, stacked[:, :, 1], precision=highest)
    new_imag = jnp.einsum('tk,tka->ta', weights_real, stacked[:, :, 1], precision=highest) + jnp.einsum('tk,tka->ta', weights_imag, stacked[:, :, 0], precision=highest)
    propagated = jnp.stack([new_real, new_imag], axis=1)
    lowered = jnp.zeros_like(propagated)
    for spin_pos in range(SPINS):
        vacant = occupation[spin_pos] == 0.0
        lowered_term = jnp.where(vacant[None, None, :], flip_spin(propagated, spin_pos), 0.0)
        lowered = jnp.where((channel == spin_pos)[:, None, None], lowered_term, lowered)
    jumped = channel < SPINS
    squared_sum = jnp.where(jumped, lax.optimization_barrier(jnp.sum(lowered * lowered, axis=(1, 2))), jnp.float32(AMPS))
    lowered = lowered * jnp.sqrt(AMPS / squared_sum)[:, None, None]
    return jnp.where(jumped[:, None, None], lowered, propagated)
```

```python
import jax
import jax.numpy as jnp
from jax import lax
from jax.experimental import pallas as pl
from jax.experimental.pallas import tpu as pltpu
from jax.sharding import PartitionSpec as P

SPINS = 19
KRYLOV = 8
LANES = 128
LANE_BITS = 7

time_step = 0.7
squarings = 8
taylor_order = 10
highest = lax.Precision.HIGHEST

CHUNK_BITS = 8
CHUNK = 1 << CHUNK_BITS
SUB = 32


def split(x):
    hi = x.astype(jnp.bfloat16)
    lo = (x - hi.astype(jnp.float32)).astype(jnp.bfloat16)
    return hi, lo


def dot(a, b):
    return jnp.dot(a, b, preferred_element_type=jnp.float32)


def fold(x):
    return jnp.sum(x.reshape(x.shape[0] // 8, 8, x.shape[1]), axis=0)


def scalar_sqrt(value):
    root = jnp.sqrt(jnp.full((8, LANES), value, jnp.float32))
    return jnp.max(root), jnp.max(1.0 / root)


def krylov_weights(a_matrix):
    size = a_matrix.shape[0]
    pad = jnp.zeros((LANES - size, LANES), jnp.float32)
    scaled = jnp.concatenate([a_matrix, pad], axis=0) * (1.0 / 2.0**squarings)
    rows = lax.broadcasted_iota(jnp.int32, (LANES, LANES), 0)
    cols = lax.broadcasted_iota(jnp.int32, (LANES, LANES), 1)
    identity = jnp.where(rows == cols, 1.0, 0.0).astype(jnp.float32)
    series = identity
    for degree in range(taylor_order, 0, -1):
        product = jnp.dot(
            scaled, series, precision=highest, preferred_element_type=jnp.float32
        )
        series = identity + product * (1.0 / degree)
    for repeat in range(squarings):
        series = jnp.dot(
            series, series, precision=highest, preferred_element_type=jnp.float32
        )
    return series


def kernel(
    channel_ref,
    couplings,
    fields,
    decays,
    state,
    out,
    basis,
    work,
    flips,
    row_table,
    lane_table,
    diag_low,
):
    node_count, _, block_rows, _ = state.shape
    rows = node_count * block_rows
    chunks = rows // CHUNK
    subs = CHUNK // SUB
    channel = channel_ref[0]
    device = lax.axis_index("amp")
    zero_tile = jnp.zeros((8, LANES), jnp.float32)
    per_block = block_rows // CHUNK

    table_shape = (CHUNK, CHUNK)
    crossed = lax.broadcasted_iota(jnp.int32, table_shape, 0)
    crossed = crossed ^ lax.broadcasted_iota(jnp.int32, table_shape, 1)
    for table, first_spin, bits in (
        (row_table, LANE_BITS, CHUNK_BITS),
        (lane_table, 0, LANE_BITS),
    ):
        value = jnp.zeros(table_shape, jnp.float32)
        for bit in range(bits):
            value = jnp.where(crossed == 1 << bit, fields[first_spin + bit], value)
        table[0], table[1] = split(value)

    low_shape = (CHUNK, LANES)
    low_pos = lax.broadcasted_iota(jnp.int32, low_shape, 0) * LANES
    low_pos = low_pos + lax.broadcasted_iota(jnp.int32, low_shape, 1)
    low_bits = LANE_BITS + CHUNK_BITS
    before = None
    low_real = jnp.zeros(low_shape, jnp.float32)
    low_imag = jnp.zeros(low_shape, jnp.float32)
    for spin in range(low_bits):
        occupied = (lax.shift_right_logical(low_pos, spin) & 1).astype(jnp.float32)
        sign = 1.0 - 2.0 * occupied
        low_imag = low_imag - 0.5 * decays[spin] * occupied
        if spin > 0:
            low_real = low_real - couplings[spin - 1] * (before * sign)
        before = sign
    diag_low[0] = low_real
    diag_low[1] = low_imag

    def high_diagonal(i):
        bits = [
            (lax.shift_right_logical(i, b) & 1).astype(jnp.float32)
            for b in range(SPINS - low_bits)
        ]
        signs = [1.0 - 2.0 * bit for bit in bits]
        real = jnp.float32(0.0)
        imag = jnp.float32(0.0)
        for b in range(len(bits)):
            imag = imag - 0.5 * decays[low_bits + b] * bits[b]
            if b > 0:
                real = real - couplings[low_bits + b - 1] * signs[b - 1] * signs[b]
        edge = couplings[low_bits - 1] * signs[0]
        return real - edge, real + edge, imag

    def start_norm(i, acc):
        node = i // per_block
        first = (i % per_block) * CHUNK
        for part in range(2):
            x = state[node, part, pl.ds(first, CHUNK), :]
            acc = acc + fold(x * x)
        return acc

    start_sq = jnp.sum(lax.fori_loop(0, chunks, start_norm, zero_tile))
    beta, inv_beta = scalar_sqrt(start_sq)

    def start_vector(i, carry):
        node = i // per_block
        first = (i % per_block) * CHUNK
        for part in range(2):
            basis[0, pl.ds(i * CHUNK, CHUNK), part * LANES : (part + 1) * LANES] = (
                state[node, part, pl.ds(first, CHUNK), :] * inv_beta
            )
        return carry

    lax.fori_loop(0, chunks, start_vector, 0)

    mat_rows = lax.broadcasted_iota(jnp.int32, (2 * KRYLOV, LANES), 0)
    mat_cols = lax.broadcasted_iota(jnp.int32, (2 * KRYLOV, LANES), 1)
    a_matrix = jnp.zeros((2 * KRYLOV, LANES), jnp.float32)

    def put(matrix, k, j, real, imag):
        a_real = time_step * imag
        a_imag = -time_step * real
        for r, c, value in (
            (k, j, a_real),
            (k, j + KRYLOV, -a_imag),
            (k + KRYLOV, j, a_imag),
            (k + KRYLOV, j + KRYLOV, a_real),
        ):
            matrix = jnp.where((mat_rows == r) & (mat_cols == c), value, matrix)
        return matrix

    high_fields = [
        fields[LANE_BITS + CHUNK_BITS + b] for b in range(SPINS - LANE_BITS - CHUNK_BITS)
    ]

    for j in range(KRYLOV):
        last = j + 1 == KRYLOV

        def apply_chunk(i, acc, j=j):
            base = pl.multiple_of(i * CHUNK, CHUNK)
            hi, lo = split(basis[j, pl.ds(base, CHUNK), :])
            flips[...] = (
                dot(row_table[0], hi)
                + dot(row_table[1], hi)
                + dot(row_table[0], lo)
                + dot(hi, lane_table[0])
                + dot(lo, lane_table[0])
                + dot(hi, lane_table[1])
            )
            acc = list(acc)
            real_vacant, real_occupied, imag_high = high_diagonal(i)
            for s in range(subs):
                here = pl.ds(base + s * SUB, SUB)
                x = basis[j, here, :]
                f = flips[s * SUB : (s + 1) * SUB, :]
                for b, field in enumerate(high_fields):
                    there = pl.multiple_of((i ^ (1 << b)) * CHUNK, CHUNK)
                    f = f + field * basis[j, pl.ds(there + s * SUB, SUB), :]
                part = slice(s * SUB, (s + 1) * SUB)
                dr = diag_low[0, part, :] + (real_vacant if s < subs // 2 else real_occupied)
                di = diag_low[1, part, :] + imag_high
                xr, xi = x[:, :LANES], x[:, LANES:]
                wr = dr * xr - di * xi - f[:, :LANES]
                wi = dr * xi + di * xr - f[:, LANES:]
                work[here, :LANES] = wr
                work[here, LANES:] = wi
                for k in range(j + 1):
                    vr = basis[k, here, :LANES]
                    vi = basis[k, here, LANES:]
                    acc[2 * k] = acc[2 * k] + fold(vr * wr + vi * wi)
                    acc[2 * k + 1] = acc[2 * k + 1] + fold(vr * wi - vi * wr)
                acc[-1] = acc[-1] + fold(wr * wr + wi * wi)
            return tuple(acc)

        sums = lax.fori_loop(0, chunks, apply_chunk, (zero_tile,) * (2 * j + 3))
        coeffs = [jnp.sum(t) for t in sums]
        for k in range(j + 1):
            a_matrix = put(a_matrix, k, j, coeffs[2 * k], coeffs[2 * k + 1])
        if last:
            break
        left = coeffs[-1]
        for value in coeffs[:-1]:
            left = left - value * value
        norm, inv_norm = scalar_sqrt(left)
        a_matrix = put(a_matrix, j + 1, j, norm, jnp.float32(0.0))

        def subtract_chunk(i, carry, j=j, coeffs=coeffs, inv_norm=inv_norm):
            base = pl.multiple_of(i * CHUNK, CHUNK)
            for s in range(subs):
                here = pl.ds(base + s * SUB, SUB)
                rr = work[here, :LANES]
                ri = work[here, LANES:]
                for k in range(j + 1):
                    vr = basis[k, here, :LANES]
                    vi = basis[k, here, LANES:]
                    hr, hm = coeffs[2 * k], coeffs[2 * k + 1]
                    rr = rr - (hr * vr - hm * vi)
                    ri = ri - (hr * vi + hm * vr)
                basis[j + 1, here, :LANES] = rr * inv_norm
                basis[j + 1, here, LANES:] = ri * inv_norm
            return carry

        lax.fori_loop(0, chunks, subtract_chunk, 0)

    series = krylov_weights(a_matrix)
    first = series[: 2 * KRYLOV, :] * beta
    weights = [
        jnp.sum(jnp.where((mat_rows == k) & (mat_cols == 0), first, 0.0))
        for k in range(2 * KRYLOV)
    ]
    sub_pos = lax.broadcasted_iota(jnp.int32, (SUB, LANES), 0) * LANES
    sub_pos = sub_pos + lax.broadcasted_iota(jnp.int32, (SUB, LANES), 1)

    def combine(i, acc):
        base = pl.multiple_of(i * CHUNK, CHUNK)
        for s in range(subs):
            here = pl.ds(base + s * SUB, SUB)
            pr = jnp.zeros((SUB, LANES), jnp.float32)
            pi = jnp.zeros((SUB, LANES), jnp.float32)
            for k in range(KRYLOV):
                vr = basis[k, here, :LANES]
                vi = basis[k, here, LANES:]
                cr, ci = weights[k], weights[k + KRYLOV]
                pr = pr + (cr * vr - ci * vi)
                pi = pi + (cr * vi + ci * vr)
            work[here, :LANES] = pr
            work[here, LANES:] = pi
            position = sub_pos + (base + s * SUB) * LANES
            occupied = lax.shift_right_logical(position, channel) & 1
            acc = acc + fold(jnp.where(occupied == 1, pr * pr + pi * pi, 0.0))
        return acc

    total = jnp.sum(lax.fori_loop(0, chunks, combine, zero_tile))
    jumped = channel < SPINS
    size = jnp.float32(rows * LANES)
    total = jnp.where(jumped, total, size)
    root = jnp.sqrt(size / jnp.full((8, LANES), total, jnp.float32))
    scale = jnp.max(root)
    in_lanes = channel < LANE_BITS
    lane_shift = jnp.where(in_lanes, lax.shift_left(1, channel), 0)
    row_shift = jnp.where(
        in_lanes | (channel >= SPINS),
        0,
        lax.shift_left(1, jnp.maximum(channel - LANE_BITS, 0)),
    )
    in_sublanes = row_shift < 8
    near = jnp.where(in_sublanes, row_shift, 0)
    far = jnp.where(in_sublanes, 0, row_shift)
    lane_turn = (LANES - lane_shift) % LANES
    row_turn = (SUB - near) % SUB

    def jump(i, carry):
        local = pl.multiple_of(i * SUB, SUB)
        base = device * block_rows + local
        source = pl.multiple_of(base + far, 8)
        position = sub_pos + base * LANES
        vacant = (lax.shift_right_logical(position, channel) & 1) == 0
        for part in range(2):
            x = work[pl.ds(source, SUB), part * LANES : (part + 1) * LANES]
            x = pltpu.roll(x, row_turn, 0)
            x = pltpu.roll(x, lane_turn, 1)
            out[part, pl.ds(local, SUB), :] = jnp.where(vacant, x * scale, 0.0)
        return carry

    lax.fori_loop(0, block_rows // SUB, jump, 0)


def body(amplitudes, couplings, fields, decays, channel):
    node_count = lax.axis_size("amp")
    local_len = amplitudes.shape[2]
    block_rows = local_len // LANES
    rows = node_count * block_rows
    vmem = pl.BlockSpec(memory_space=pltpu.VMEM)
    smem = pl.BlockSpec(memory_space=pltpu.SMEM)
    call = pl.pallas_call(
        kernel,
        out_shape=jax.ShapeDtypeStruct((2, block_rows, LANES), jnp.float32),
        in_specs=[smem] * 4 + [vmem],
        out_specs=vmem,
        scratch_shapes=[
            pltpu.VMEM((KRYLOV, rows, 2 * LANES), jnp.float32),
            pltpu.VMEM((rows + rows // 2, 2 * LANES), jnp.float32),
            pltpu.VMEM((CHUNK, 2 * LANES), jnp.float32),
            pltpu.VMEM((2, CHUNK, CHUNK), jnp.bfloat16),
            pltpu.VMEM((2, CHUNK, CHUNK), jnp.bfloat16),
            pltpu.VMEM((2, CHUNK, LANES), jnp.float32),
        ],
        compiler_params=pltpu.CompilerParams(vmem_limit_bytes=62 * 1024 * 1024),
        name="trajectory",
    )
    results = []
    for t in range(amplitudes.shape[0]):
        block = amplitudes[t].reshape(2, block_rows, LANES)
        state = lax.all_gather(block, "amp")
        results.append(call(channel[t : t + 1], couplings, fields, decays, state))
    return jnp.stack(results).reshape(amplitudes.shape)


def solution(mesh):
    placed = (P("traj", None, "amp"), P(), P(), P(), P("traj"))
    return jax.shard_map(
        body, mesh=mesh, in_specs=placed, out_specs=P("traj", None, "amp"), check_vma=False
    )
```

```python
import jax
import jax.numpy as jnp
from jax import lax
from jax.experimental import pallas as pl
from jax.experimental.pallas import tpu as pltpu
from jax.sharding import PartitionSpec as P

SPINS = 19
KRYLOV = 8
LANES = 128
LANE_BITS = 7

time_step = 0.7
squarings = 8
taylor_order = 10
highest = lax.Precision.HIGHEST

CHUNK_BITS = 8
CHUNK = 1 << CHUNK_BITS
SUB = 32


def split(x):
    hi = x.astype(jnp.bfloat16)
    lo = (x - hi.astype(jnp.float32)).astype(jnp.bfloat16)
    return hi, lo


def dot(a, b):
    return jnp.dot(a, b, preferred_element_type=jnp.float32)


def fold(x):
    return jnp.sum(x.reshape(x.shape[0] // 8, 8, x.shape[1]), axis=0)


def scalar_sqrt(value):
    root = jnp.sqrt(jnp.full((8, LANES), value, jnp.float32))
    return jnp.max(root), jnp.max(1.0 / root)


def krylov_weights(a_matrix):
    size = a_matrix.shape[0]
    pad = jnp.zeros((LANES - size, LANES), jnp.float32)
    scaled = jnp.concatenate([a_matrix, pad], axis=0) * (1.0 / 2.0**squarings)
    rows = lax.broadcasted_iota(jnp.int32, (LANES, LANES), 0)
    cols = lax.broadcasted_iota(jnp.int32, (LANES, LANES), 1)
    identity = jnp.where(rows == cols, 1.0, 0.0).astype(jnp.float32)
    series = identity
    for degree in range(taylor_order, 0, -1):
        product = jnp.dot(
            scaled, series, precision=highest, preferred_element_type=jnp.float32
        )
        series = identity + product * (1.0 / degree)
    for repeat in range(squarings):
        series = jnp.dot(
            series, series, precision=highest, preferred_element_type=jnp.float32
        )
    return series


def kernel(
    channel_ref,
    couplings,
    fields,
    decays,
    state,
    out,
    basis,
    work,
    flips,
    row_table,
    lane_table,
    diag_low,
):
    node_count, _, block_rows, _ = state.shape
    rows = node_count * block_rows
    chunks = rows // CHUNK
    subs = CHUNK // SUB
    channel = channel_ref[0]
    device = lax.axis_index("amp")
    zero_tile = jnp.zeros((8, LANES), jnp.float32)
    per_block = block_rows // CHUNK

    table_shape = (CHUNK, CHUNK)
    crossed = lax.broadcasted_iota(jnp.int32, table_shape, 0)
    crossed = crossed ^ lax.broadcasted_iota(jnp.int32, table_shape, 1)
    for table, first_spin, bits in (
        (row_table, LANE_BITS, CHUNK_BITS),
        (lane_table, 0, LANE_BITS),
    ):
        value = jnp.zeros(table_shape, jnp.float32)
        for bit in range(bits):
            value = jnp.where(crossed == 1 << bit, fields[first_spin + bit], value)
        table[0], table[1] = split(value)

    low_shape = (CHUNK, LANES)
    low_pos = lax.broadcasted_iota(jnp.int32, low_shape, 0) * LANES
    low_pos = low_pos + lax.broadcasted_iota(jnp.int32, low_shape, 1)
    low_bits = LANE_BITS + CHUNK_BITS
    before = None
    low_real = jnp.zeros(low_shape, jnp.float32)
    low_imag = jnp.zeros(low_shape, jnp.float32)
    for spin in range(low_bits):
        occupied = (lax.shift_right_logical(low_pos, spin) & 1).astype(jnp.float32)
        sign = 1.0 - 2.0 * occupied
        low_imag = low_imag - 0.5 * decays[spin] * occupied
        if spin > 0:
            low_real = low_real - couplings[spin - 1] * (before * sign)
        before = sign
    diag_low[0] = low_real
    diag_low[1] = low_imag

    def high_diagonal(i):
        bits = [
            (lax.shift_right_logical(i, b) & 1).astype(jnp.float32)
            for b in range(SPINS - low_bits)
        ]
        signs = [1.0 - 2.0 * bit for bit in bits]
        real = jnp.float32(0.0)
        imag = jnp.float32(0.0)
        for b in range(len(bits)):
            imag = imag - 0.5 * decays[low_bits + b] * bits[b]
            if b > 0:
                real = real - couplings[low_bits + b - 1] * signs[b - 1] * signs[b]
        edge = couplings[low_bits - 1] * signs[0]
        return real - edge, real + edge, imag

    def start_norm(i, acc):
        node = i // per_block
        first = (i % per_block) * CHUNK
        for part in range(2):
            x = state[node, part, pl.ds(first, CHUNK), :]
            acc = acc + fold(x * x)
        return acc

    start_sq = jnp.sum(lax.fori_loop(0, chunks, start_norm, zero_tile))
    beta, inv_beta = scalar_sqrt(start_sq)

    def start_vector(i, carry):
        node = i // per_block
        first = (i % per_block) * CHUNK
        for part in range(2):
            basis[0, pl.ds(i * CHUNK, CHUNK), part * LANES : (part + 1) * LANES] = (
                state[node, part, pl.ds(first, CHUNK), :] * inv_beta
            )
        return carry

    lax.fori_loop(0, chunks, start_vector, 0)

    mat_rows = lax.broadcasted_iota(jnp.int32, (2 * KRYLOV, LANES), 0)
    mat_cols = lax.broadcasted_iota(jnp.int32, (2 * KRYLOV, LANES), 1)
    a_matrix = jnp.zeros((2 * KRYLOV, LANES), jnp.float32)

    def put(matrix, k, j, real, imag):
        a_real = time_step * imag
        a_imag = -time_step * real
        for r, c, value in (
            (k, j, a_real),
            (k, j + KRYLOV, -a_imag),
            (k + KRYLOV, j, a_imag),
            (k + KRYLOV, j + KRYLOV, a_real),
        ):
            matrix = jnp.where((mat_rows == r) & (mat_cols == c), value, matrix)
        return matrix

    high_fields = [
        fields[LANE_BITS + CHUNK_BITS + b] for b in range(SPINS - LANE_BITS - CHUNK_BITS)
    ]

    for j in range(KRYLOV):
        last = j + 1 == KRYLOV

        def apply_chunk(i, acc, j=j):
            base = pl.multiple_of(i * CHUNK, CHUNK)
            hi, lo = split(basis[j, pl.ds(base, CHUNK), :])
            flips[...] = (
                dot(row_table[0], hi)
                + dot(row_table[1], hi)
                + dot(row_table[0], lo)
                + dot(hi, lane_table[0])
                + dot(lo, lane_table[0])
                + dot(hi, lane_table[1])
            )
            acc = list(acc)
            real_vacant, real_occupied, imag_high = high_diagonal(i)
            for s in range(subs):
                here = pl.ds(base + s * SUB, SUB)
                x = basis[j, here, :]
                f = flips[s * SUB : (s + 1) * SUB, :]
                for b, field in enumerate(high_fields):
                    there = pl.multiple_of((i ^ (1 << b)) * CHUNK, CHUNK)
                    f = f + field * basis[j, pl.ds(there + s * SUB, SUB), :]
                part = slice(s * SUB, (s + 1) * SUB)
                dr = diag_low[0, part, :] + (real_vacant if s < subs // 2 else real_occupied)
                di = diag_low[1, part, :] + imag_high
                xr, xi = x[:, :LANES], x[:, LANES:]
                wr = dr * xr - di * xi - f[:, :LANES]
                wi = dr * xi + di * xr - f[:, LANES:]
                work[here, :LANES] = wr
                work[here, LANES:] = wi
                for k in range(j + 1):
                    vr = basis[k, here, :LANES]
                    vi = basis[k, here, LANES:]
                    acc[2 * k] = acc[2 * k] + fold(vr * wr + vi * wi)
                    acc[2 * k + 1] = acc[2 * k + 1] + fold(vr * wi - vi * wr)
                acc[-1] = acc[-1] + fold(wr * wr + wi * wi)
            return tuple(acc)

        sums = lax.fori_loop(0, chunks, apply_chunk, (zero_tile,) * (2 * j + 3))
        coeffs = [jnp.sum(t) for t in sums]
        for k in range(j + 1):
            a_matrix = put(a_matrix, k, j, coeffs[2 * k], coeffs[2 * k + 1])
        if last:
            break
        left = coeffs[-1]
        for value in coeffs[:-1]:
            left = left - value * value
        norm, inv_norm = scalar_sqrt(left)
        a_matrix = put(a_matrix, j + 1, j, norm, jnp.float32(0.0))

        def subtract_chunk(i, carry, j=j, coeffs=coeffs, inv_norm=inv_norm):
            base = pl.multiple_of(i * CHUNK, CHUNK)
            for s in range(subs):
                here = pl.ds(base + s * SUB, SUB)
                rr = work[here, :LANES]
                ri = work[here, LANES:]
                for k in range(j + 1):
                    vr = basis[k, here, :LANES]
                    vi = basis[k, here, LANES:]
                    hr, hm = coeffs[2 * k], coeffs[2 * k + 1]
                    rr = rr - (hr * vr - hm * vi)
                    ri = ri - (hr * vi + hm * vr)
                basis[j + 1, here, :LANES] = rr * inv_norm
                basis[j + 1, here, LANES:] = ri * inv_norm
            return carry

        lax.fori_loop(0, chunks, subtract_chunk, 0)

    series = krylov_weights(a_matrix)
    first = series[: 2 * KRYLOV, :] * beta
    weights = [
        jnp.sum(jnp.where((mat_rows == k) & (mat_cols == 0), first, 0.0))
        for k in range(2 * KRYLOV)
    ]
    sub_pos = lax.broadcasted_iota(jnp.int32, (SUB, LANES), 0) * LANES
    sub_pos = sub_pos + lax.broadcasted_iota(jnp.int32, (SUB, LANES), 1)

    def combine(i, acc):
        base = pl.multiple_of(i * CHUNK, CHUNK)
        for s in range(subs):
            here = pl.ds(base + s * SUB, SUB)
            pr = jnp.zeros((SUB, LANES), jnp.float32)
            pi = jnp.zeros((SUB, LANES), jnp.float32)
            for k in range(KRYLOV):
                vr = basis[k, here, :LANES]
                vi = basis[k, here, LANES:]
                cr, ci = weights[k], weights[k + KRYLOV]
                pr = pr + (cr * vr - ci * vi)
                pi = pi + (cr * vi + ci * vr)
            work[here, :LANES] = pr
            work[here, LANES:] = pi
            position = sub_pos + (base + s * SUB) * LANES
            occupied = lax.shift_right_logical(position, channel) & 1
            acc = acc + fold(jnp.where(occupied == 1, pr * pr + pi * pi, 0.0))
        return acc

    total = jnp.sum(lax.fori_loop(0, chunks, combine, zero_tile))
    jumped = channel < SPINS
    size = jnp.float32(rows * LANES)
    total = jnp.where(jumped, total, size)
    root = jnp.sqrt(size / jnp.full((8, LANES), total, jnp.float32))
    scale = jnp.max(root)
    in_lanes = channel < LANE_BITS
    lane_shift = jnp.where(in_lanes, lax.shift_left(1, channel), 0)
    row_shift = jnp.where(
        in_lanes | (channel >= SPINS),
        0,
        lax.shift_left(1, jnp.maximum(channel - LANE_BITS, 0)),
    )
    in_sublanes = row_shift < 8
    near = jnp.where(in_sublanes, row_shift, 0)
    far = jnp.where(in_sublanes, 0, row_shift)
    lane_turn = (LANES - lane_shift) % LANES
    row_turn = (SUB - near) % SUB

    def jump(i, carry):
        local = pl.multiple_of(i * SUB, SUB)
        base = device * block_rows + local
        source = pl.multiple_of(base + far, 8)
        position = sub_pos + base * LANES
        vacant = (lax.shift_right_logical(position, channel) & 1) == 0
        for part in range(2):
            x = work[pl.ds(source, SUB), part * LANES : (part + 1) * LANES]
            x = pltpu.roll(x, row_turn, 0)
            x = pltpu.roll(x, lane_turn, 1)
            out[part, pl.ds(local, SUB), :] = jnp.where(vacant, x * scale, 0.0)
        return carry

    lax.fori_loop(0, block_rows // SUB, jump, 0)


def gather_kernel(block, out, send_sem, recv_sem):
    me = lax.axis_index("amp")
    near = (me ^ 1, me ^ 2)
    barrier = pltpu.get_barrier_semaphore()
    for partner in near:
        pl.semaphore_signal(
            barrier, inc=1, device_id={"amp": partner}, device_id_type=pl.DeviceIdType.MESH
        )
    pl.semaphore_wait(barrier, 2)

    def copy(source, owner, part, axis, slot):
        return pltpu.make_async_remote_copy(
            src_ref=source,
            dst_ref=out.at[owner, part],
            send_sem=send_sem.at[slot],
            recv_sem=recv_sem.at[slot],
            device_id={"amp": near[axis]},
            device_id_type=pl.DeviceIdType.MESH,
        )

    direct = {}
    for turn in range(2):
        for axis in range(2):
            part = axis ^ turn
            direct[axis, part] = copy(block.at[part], me, part, axis, 2 * axis + part)
            direct[axis, part].start()
    out[me] = block[...]
    forwards = []
    for axis in range(2):
        direct[axis, axis].wait_recv()
        owner = near[axis]
        forward = copy(out.at[owner, axis], owner, axis, 1 - axis, 4 + axis)
        forward.start()
        forwards.append(forward)
    for axis in range(2):
        direct[axis, 1 - axis].wait_recv()
    for forward in forwards:
        forward.wait_recv()
    for sent in list(direct.values()) + forwards:
        sent.wait_send()


def gather(block):
    node_count = lax.axis_size("amp")
    if node_count != 4:
        return lax.all_gather(block, "amp")
    vmem = pl.BlockSpec(memory_space=pltpu.VMEM)
    return pl.pallas_call(
        gather_kernel,
        out_shape=jax.ShapeDtypeStruct((node_count,) + block.shape, block.dtype),
        in_specs=[vmem],
        out_specs=vmem,
        scratch_shapes=[pltpu.SemaphoreType.DMA((6,)), pltpu.SemaphoreType.DMA((6,))],
        compiler_params=pltpu.CompilerParams(collective_id=0, has_side_effects=True),
        name="gather",
    )(block)


def body(amplitudes, couplings, fields, decays, channel):
    node_count = lax.axis_size("amp")
    local_len = amplitudes.shape[2]
    block_rows = local_len // LANES
    rows = node_count * block_rows
    vmem = pl.BlockSpec(memory_space=pltpu.VMEM)
    smem = pl.BlockSpec(memory_space=pltpu.SMEM)
    call = pl.pallas_call(
        kernel,
        out_shape=jax.ShapeDtypeStruct((2, block_rows, LANES), jnp.float32),
        in_specs=[smem] * 4 + [vmem],
        out_specs=vmem,
        scratch_shapes=[
            pltpu.VMEM((KRYLOV, rows, 2 * LANES), jnp.float32),
            pltpu.VMEM((rows + rows // 2, 2 * LANES), jnp.float32),
            pltpu.VMEM((CHUNK, 2 * LANES), jnp.float32),
            pltpu.VMEM((2, CHUNK, CHUNK), jnp.bfloat16),
            pltpu.VMEM((2, CHUNK, CHUNK), jnp.bfloat16),
            pltpu.VMEM((2, CHUNK, LANES), jnp.float32),
        ],
        compiler_params=pltpu.CompilerParams(vmem_limit_bytes=62 * 1024 * 1024),
        name="trajectory",
    )
    results = []
    for t in range(amplitudes.shape[0]):
        block = amplitudes[t].reshape(2, block_rows, LANES)
        state = gather(block)
        results.append(call(channel[t : t + 1], couplings, fields, decays, state))
    return jnp.stack(results).reshape(amplitudes.shape)


def solution(mesh):
    placed = (P("traj", None, "amp"), P(), P(), P(), P("traj"))
    return jax.shard_map(
        body, mesh=mesh, in_specs=placed, out_specs=P("traj", None, "amp"), check_vma=False
    )
```
